128 devices in a mesh: sa: 4 (over x), sb: 2 (over core), sc: 16 (over z, y).
Axes of the slice: x: 4, y: 4, z: 4, core: 2. Of those that a mesh axis runs over, the one named last changes fastest.
Arguments:
- queries: float32 [65536, 2048], P(('sa', 'sb', 'sc')), may hold values from -6 to 6
- key_rows: float32 [65536, 2048], P(('sa', 'sb', 'sc')), may hold values from -6 to 6
- value_rows: float32 [65536, 2048], P(('sa', 'sb', 'sc')), may hold values from -6 to 6
- out_grad: float32 [65536, 2048], P(('sa', 'sb', 'sc')), may hold values from -6 to 6
- prefix_state: float32 [16, 128, 128], replicated, may hold values from -1536 to 1536
- suffix_state: float32 [16, 128, 128], replicated, may hold values from -1536 to 1536
Outputs:
- query_grad: bfloat16 [65536, 2048], P(('sa', 'sb', 'sc'))
- key_grad: bfloat16 [65536, 2048], P(('sa', 'sb', 'sc'))
- value_grad: bfloat16 [65536, 2048], P(('sa', 'sb', 'sc'))
The draws below stay inside these ranges and needn't reach their ends.
All inputs are finite; a program needn't handle non-finite values.
Results may differ from the reference program's by a relative error of at most 0.0019.
Values sent between devices are 32-bit elements; how exact they have to be, the bound alone decides.
A program may use at most 576 MiB of HBM per device.

```python
import math
import jax
import jax.numpy as jnp
from jax import lax

H = 16
E = 128
TOK_DEV = 512
TOKENS = 65536


def shard_levels(stream_key, shape, cuts, least, top_value):
    level, own = 1.0, jax.random.fold_in(stream_key, 6)
    for dim, blocks in cuts:
        steps = jnp.exp(jax.random.uniform(jax.random.fold_in(own, dim), (blocks,), jnp.float32, least / len(cuts), top_value / len(cuts)))
        level = level * jnp.repeat(steps, shape[dim] // blocks).reshape([-1 if axis == dim else 1 for axis in range(len(shape))])
    return level


def gaussian(own_key, shape, scale, reach, cuts=(), kind=jnp.bfloat16):
    entries = jax.random.normal(own_key, shape, jnp.float32) * scale
    if len(cuts) > 0:
        entries = shard_levels(own_key, shape, cuts, -0.22, 0.18) * entries
    return jnp.clip(entries, min=-reach, max=reach).astype(kind)


def setup_inputs(seed: int = 0) -> dict:
    key_list = jax.random.split(jax.random.key(seed), 7)
    queries = gaussian(key_list[0], (TOKENS, H * E), 1.0, 6.0, ((0, 128),), jnp.float32)
    key_rows = gaussian(key_list[1], (TOKENS, H * E), 1.0, 6.0, ((0, 128),), jnp.float32)
    value_rows = gaussian(key_list[2], (TOKENS, H * E), 1.0, 6.0, ((0, 128),), jnp.float32)
    out_grad = gaussian(key_list[3], (TOKENS, H * E), 1.0, 6.0, ((0, 128),), jnp.float32)
    prefix_state = gaussian(key_list[4], (H, E, E), (TOKENS ** 0.5), 1536.0, (), jnp.float32)
    suffix_state = gaussian(key_list[5], (H, E, E), (TOKENS ** 0.5), 1536.0, (), jnp.float32)
    return dict(queries=queries, key_rows=key_rows, value_rows=value_rows, out_grad=out_grad, prefix_state=prefix_state, suffix_state=suffix_state)


def block_grads(query_t, key_t, value_t, grad_t, state_before, state_after, factor):
    count = query_t.shape[0]
    highest = lax.Precision.HIGHEST
    lower = (lax.broadcasted_iota(jnp.int32, (count, count), 0) >= lax.broadcasted_iota(jnp.int32, (count, count), 1)).astype(query_t.dtype)
    grad_scores = jnp.einsum('the,she->hts', grad_t, value_t, precision=highest) * lower
    attn_scores = jnp.einsum('thd,shd->hts', query_t, key_t, precision=highest) * lower
    query_grad = factor * (jnp.einsum('the,hde->thd', grad_t, state_before, precision=highest) + jnp.einsum('hts,shd->thd', grad_scores, key_t, precision=highest))
    key_grad = factor * (jnp.einsum('she,hed->shd', value_t, state_after, precision=highest) + jnp.einsum('hts,thd->shd', grad_scores, query_t, precision=highest))
    value_grad = factor * (jnp.einsum('shd,hed->she', key_t, state_after, precision=highest) + jnp.einsum('hts,the->she', attn_scores, grad_t, precision=highest))
    return (query_grad.astype(jnp.bfloat16), key_grad.astype(jnp.bfloat16), value_grad.astype(jnp.bfloat16))

def reference(queries, key_rows, value_rows, out_grad, prefix_state, suffix_state):
    block_count = TOKENS // TOK_DEV
    shaped = (block_count, TOK_DEV, H, E)
    query_blocks = queries.reshape(shaped)
    key_blocks = key_rows.reshape(shaped)
    value_blocks = value_rows.reshape(shaped)
    grad_blocks = out_grad.reshape(shaped)
    highest = lax.Precision.HIGHEST
    factor = 1.0 / math.sqrt(E * TOKENS)

    def local_terms(pieces):
        key_t, value_t, grad_t, query_t = pieces
        return (jnp.einsum('thd,the->hde', key_t, value_t, precision=highest), jnp.einsum('the,thd->hed', grad_t, query_t, precision=highest))
    kv_all, grad_all = lax.map(local_terms, (key_blocks, value_blocks, grad_blocks, query_blocks))

    def carry_step(carry, term):
        return (carry + term, carry)
    final_forward, before_all = lax.scan(carry_step, prefix_state, kv_all)
    final_backward, after_all = lax.scan(carry_step, suffix_state, grad_all, reverse=True)

    def one_block(pieces):
        query_t, key_t, value_t, grad_t, state_before, state_after = pieces
        return block_grads(query_t, key_t, value_t, grad_t, state_before, state_after, factor)
    query_grad, key_grad, value_grad = lax.map(one_block, (query_blocks, key_blocks, value_blocks, grad_blocks, before_all, after_all))
    return (query_grad.reshape(TOKENS, H * E), key_grad.reshape(TOKENS, H * E), value_grad.reshape(TOKENS, H * E))
```

```python
import functools
import math

import jax
import jax.numpy as jnp
from jax import lax
from jax.experimental import pallas as pl
from jax.experimental.pallas import tpu as pltpu
from jax.sharding import PartitionSpec as P

MESH = pl.DeviceIdType.MESH
F32 = jnp.float32
BF16 = jnp.bfloat16
SEGMENTS = (4, 4, 4, 4)


def split2(x):
    hi = x.astype(BF16)
    lo = (x - hi.astype(F32)).astype(BF16)
    return jnp.concatenate([hi, lo], axis=1)


def halves(x):
    hi = x.astype(BF16)
    lo = (x - hi.astype(F32)).astype(BF16)
    return hi, lo


def mm(a, b):
    return jnp.dot(a, b, preferred_element_type=F32)


def mm_nt(a, b):
    return lax.dot_general(a, b, (((1,), (1,)), ((), ())), preferred_element_type=F32)


def fold_columns(r):
    n = r.shape[1] // 2
    return r[:, :n] + r[:, n:]


def fold_rows(r):
    n = r.shape[0] // 2
    return r[:n] + r[n:]


def scores(a2, b2):
    e = a2.shape[1] // 2
    swapped = jnp.concatenate([b2[:, e:], b2[:, :e]], axis=1)
    return mm_nt(
        jnp.concatenate([a2, a2], axis=1), jnp.concatenate([b2, swapped], axis=1)
    )


def kernel(
    axes, factor,
    q_hbm, k_hbm, v_hbm, g_hbm, prefix_hbm, suffix_hbm,
    qg_hbm, kg_hbm, vg_hbm,
    q2, k2, v2, g2, qt, gt, acc_q, acc_k, acc_v, land_q,
    local, gathered, totals, entering, ends, stage,
    load_sem, end_sem, in_send, in_recv, tot_send, tot_recv, out_send, out_recv, store_sem,
):
    nx, nc, ns = axes
    groups = nx * nc
    sa, sb, sc = lax.axis_index("sa"), lax.axis_index("sb"), lax.axis_index("sc")
    group = sa * nc + sb
    heads, rows, e = acc_q.shape
    half = rows // 2

    def peer(j):
        return (sa, sb, j)

    def group_peer(g):
        return (g // nc, lax.rem(g, nc), sc)

    landing = ((k_hbm, acc_q), (v_hbm, acc_k), (g_hbm, acc_v), (q_hbm, land_q))

    def load(a, h):
        src, dst = landing[a]
        return pltpu.make_async_copy(
            src.at[:, pl.ds(pl.multiple_of(h * e, e), e)], dst.at[h], load_sem.at[a, h]
        )

    def head_at(i):
        return lax.rem(sc + 1 + i, ns)

    for pair in ((0, 1), (2, 3)):
        @pl.loop(0, heads)
        def _(i):
            for a in pair:
                load(a, head_at(i)).start()

    end_copies = [
        pltpu.make_async_copy(prefix_hbm.at[sc], ends.at[0], end_sem.at[0]),
        pltpu.make_async_copy(suffix_hbm.at[sc], ends.at[1], end_sem.at[1]),
    ]
    for c in end_copies:
        c.start()

    barrier = pltpu.get_barrier_semaphore()

    @pl.loop(1, ns)
    def _(i):
        pl.semaphore_signal(barrier, inc=1, device_id=peer(lax.rem(sc + i, ns)), device_id_type=MESH)

    @pl.loop(1, groups)
    def _(i):
        pl.semaphore_signal(barrier, inc=1, device_id=group_peer(lax.rem(group + i, groups)), device_id_type=MESH)

    pl.semaphore_wait(barrier, ns - 1 + groups - 1)

    def in_copy(w, head, source, target):
        return pltpu.make_async_remote_copy(
            src_ref=local.at[w, head], dst_ref=gathered.at[w, source],
            send_sem=in_send.at[w, head], recv_sem=in_recv.at[w, source],
            device_id=peer(target), device_id_type=MESH,
        )

    def total_copy(w, source, target):
        return pltpu.make_async_remote_copy(
            src_ref=totals.at[w, source], dst_ref=totals.at[w, source],
            send_sem=tot_send.at[w, target], recv_sem=tot_recv.at[w, source],
            device_id=group_peer(target), device_id_type=MESH,
        )

    def out_copy(w, head, target):
        return pltpu.make_async_remote_copy(
            src_ref=gathered.at[w, target], dst_ref=entering.at[w, head],
            send_sem=out_send.at[w, target], recv_sem=out_recv.at[w, head],
            device_id=peer(target), device_id_type=MESH,
        )

    def local_sum(w, left, right, left_t, left2, right2):
        @pl.loop(0, heads)
        def _(i):
            h = head_at(i)
            a, b = left, right
            load(a, h).wait()
            load(b, h).wait()
            x2 = split2(landing[a][1][h])
            y2 = split2(landing[b][1][h])
            left2[h] = x2
            right2[h] = y2
            xt = x2.T
            if left_t is not None:
                left_t[h] = xt
            local[w, h] = fold_columns(fold_rows(mm(xt, y2)))

            @pl.when(h != sc)
            def _():
                in_copy(w, h, sc, h).start()

    local_sum(0, 1, 0, None, v2, k2)
    local_sum(1, 2, 3, gt, g2, q2)

    lower = lax.broadcasted_iota(jnp.int32, (half, half), 0) >= lax.broadcasted_iota(
        jnp.int32, (half, half), 1
    )

    def within_block(h):
        qt[h] = q2[h].T
        top, low = pl.ds(0, half), pl.ds(half, half)

        def three(a2, b2):
            s00 = jnp.where(lower, scores(a2[h, top, :], b2[h, top, :]), 0.0)
            s10 = scores(a2[h, low, :], b2[h, top, :])
            s11 = jnp.where(lower, scores(a2[h, low, :], b2[h, low, :]), 0.0)
            return halves(s00), halves(s10), halves(s11)

        def transposed(xt, parts):
            (h00, l00), (h10, l10), (h11, l11) = parts
            x = xt[h]
            first = mm(
                jnp.concatenate([x, x], axis=1),
                jnp.concatenate([h00, h10, l00, l10], axis=0),
            )
            y = x[:, half:]
            second = mm(
                jnp.concatenate([y, y], axis=1), jnp.concatenate([h11, l11], axis=0)
            )
            return fold_rows(first).T, fold_rows(second).T

        parts = three(g2, v2)
        (h00, l00), (h10, l10), (h11, l11) = parts
        kk = k2[h]
        acc_q[h, top, :] = fold_columns(
            fold_rows(mm(jnp.concatenate([h00, l00], axis=0), kk[:half]))
        )
        wide = jnp.concatenate(
            [jnp.concatenate([h10, h11], axis=1), jnp.concatenate([l10, l11], axis=1)],
            axis=0,
        )
        acc_q[h, low, :] = fold_columns(fold_rows(mm(wide, kk)))
        first, second = transposed(qt, parts)
        acc_k[h, top, :] = first
        acc_k[h, low, :] = second
        first, second = transposed(gt, three(q2, k2))
        acc_v[h, top, :] = first
        acc_v[h, low, :] = second

    def segment(start, count):
        @pl.loop(start, start + count)
        def _(h):
            within_block(h)

    def send_totals(w):
        gathered[w, sc] = local[w, sc]

        @pl.loop(1, ns)
        def _(i):
            j = lax.rem(sc + i, ns)
            in_copy(w, j, j, j).wait_recv()

        total = gathered[w, 0]
        for j in range(1, ns):
            total = total + gathered[w, j]
        totals[w, group] = total

        @pl.loop(1, groups)
        def _(i):
            total_copy(w, group, lax.rem(group + i, groups)).start()

    def send_states(w):
        @pl.loop(1, groups)
        def _(i):
            g = lax.rem(group + i, groups)
            total_copy(w, g, g).wait_recv()

        end_copies[w].wait()
        state = ends[w]
        if w == 0:
            state = state.T
        for g in range(groups):
            use = g < group if w == 0 else g > group
            state = state + jnp.where(use, totals[w, g], 0.0)
        for j in range(ns) if w == 0 else reversed(range(ns)):
            term = gathered[w, j]
            gathered[w, j] = state
            state = state + term
        entering[w, sc] = gathered[w, sc]

        @pl.loop(1, ns)
        def _(i):
            out_copy(w, sc, lax.rem(sc + i, ns)).start()

    done = 0
    for count, step in zip(
        SEGMENTS,
        (
            functools.partial(send_totals, 0),
            functools.partial(send_states, 0),
            functools.partial(send_totals, 1),
            functools.partial(send_states, 1),
        ),
    ):
        segment(done, count)
        done += count
        step()

    def store(o, h):
        dst = (qg_hbm, kg_hbm, vg_hbm)[o]
        return pltpu.make_async_copy(
            stage.at[o, h], dst.at[:, pl.ds(pl.multiple_of(h * e, e), e)], store_sem.at[o, h]
        )

    def finish(o, h, x2, acc, state):
        s2 = split2(state)
        r = fold_columns(mm(x2[h], jnp.concatenate([s2, s2], axis=0)))
        stage[o, h] = ((r + acc[h]) * factor).astype(BF16)
        store(o, h).start()

    def arrived(w, i):
        h = lax.rem(sc - i + ns, ns)

        @pl.when(i > 0)
        def _():
            out_copy(w, h, h).wait_recv()

        return h

    @pl.loop(0, heads)
    def _(i):
        h = arrived(0, i)
        finish(0, h, g2, acc_q, entering[0, h])

    @pl.loop(0, heads)
    def _(i):
        h = arrived(1, i)
        state = entering[1, h]
        finish(1, h, v2, acc_k, state)
        finish(2, h, k2, acc_v, state.T)

    for w in range(2):
        @pl.loop(1, ns)
        def _(i):
            j = lax.rem(sc + i, ns)
            in_copy(w, j, sc, j).wait_send()
            out_copy(w, sc, j).wait_send()

        @pl.loop(1, groups)
        def _(i):
            total_copy(w, group, lax.rem(group + i, groups)).wait_send()

    @pl.loop(0, heads)
    def _(h):
        for o in range(3):
            store(o, h).wait()


def shards(axes, queries, key_rows, value_rows, out_grad, prefix_state, suffix_state):
    rows = queries.shape[0]
    heads, e, _ = prefix_state.shape
    nx, nc, ns = axes
    groups = nx * nc
    factor = 1.0 / math.sqrt(e * rows * groups * ns)
    hbm = pl.BlockSpec(memory_space=pl.ANY)
    dma = pltpu.SemaphoreType.DMA
    out = jax.ShapeDtypeStruct((rows, heads * e), BF16)
    pair = pltpu.VMEM((heads, rows, 2 * e), BF16)
    pair_t = pltpu.VMEM((heads, 2 * e, rows), BF16)
    wide = pltpu.VMEM((heads, rows, e), F32)
    states = pltpu.VMEM((2, heads, e, e), F32)
    return pl.pallas_call(
        functools.partial(kernel, axes, factor),
        out_shape=(out, out, out),
        in_specs=[hbm] * 6,
        out_specs=(hbm, hbm, hbm),
        scratch_shapes=[
            pair, pair, pair, pair, pair_t, pair_t,
            wide, wide, wide, wide,
            states, states, pltpu.VMEM((2, groups, e, e), F32), states,
            pltpu.VMEM((2, e, e), F32),
            pltpu.VMEM((3, heads, rows, e), BF16),
            dma((4, heads)), dma((2,)),
            dma((2, ns)), dma((2, ns)),
            dma((2, groups)), dma((2, groups)),
            dma((2, ns)), dma((2, ns)),
            dma((3, heads)),
        ],
        compiler_params=pltpu.CompilerParams(
            collective_id=0, has_side_effects=True, vmem_limit_bytes=60 << 20
        ),
    )(queries, key_rows, value_rows, out_grad, prefix_state, suffix_state)


def solution(mesh):
    axes = tuple(mesh.shape[name] for name in ("sa", "sb", "sc"))
    split = P(("sa", "sb", "sc"), None)
    return jax.shard_map(
        functools.partial(shards, axes),
        mesh=mesh,
        in_specs=(split, split, split, split, P(), P()),
        out_specs=(split, split, split),
        check_vma=False,
    )
```

```python
import functools
import math

import jax
import jax.numpy as jnp
from jax import lax
from jax.experimental import pallas as pl
from jax.experimental.pallas import tpu as pltpu
from jax.sharding import PartitionSpec as P

MESH = pl.DeviceIdType.MESH
F32 = jnp.float32
BF16 = jnp.bfloat16
SEGMENTS = (1, 2, 6, 1, 6)


def split2(x):
    hi = x.astype(BF16)
    lo = (x - hi.astype(F32)).astype(BF16)
    return jnp.concatenate([hi, lo], axis=1)


def halves(x):
    hi = x.astype(BF16)
    lo = (x - hi.astype(F32)).astype(BF16)
    return hi, lo


def mm(a, b):
    return jnp.dot(a, b, preferred_element_type=F32)


def mm_nt(a, b):
    return lax.dot_general(a, b, (((1,), (1,)), ((), ())), preferred_element_type=F32)


def fold_columns(r):
    n = r.shape[1] // 2
    return r[:, :n] + r[:, n:]


def fold_rows(r):
    n = r.shape[0] // 2
    return r[:n] + r[n:]


def scores(a2, b2):
    e = a2.shape[1] // 2
    swapped = jnp.concatenate([b2[:, e:], b2[:, :e]], axis=1)
    return mm_nt(
        jnp.concatenate([a2, a2], axis=1), jnp.concatenate([b2, swapped], axis=1)
    )


def finish(factor, x2, acc, state):
    s2 = split2(state)
    r = fold_columns(mm(x2, jnp.concatenate([s2, s2], axis=0)))
    return ((r + acc) * factor).astype(BF16)


def kernel(
    axes, factor,
    q_hbm, k_hbm, v_hbm, g_hbm, prefix_hbm, suffix_hbm,
    k2, v2, acc_k, acc_v, after, qg,
    q2, g2, qt, gt, acc_q, land_q,
    local, gathered, totals, before, ends,
    load_sem, end_sem, in_send, in_recv, tot_send, tot_recv, out_send, out_recv,
):
    nx, nc, ns = axes
    groups = nx * nc
    sa, sb, sc = lax.axis_index("sa"), lax.axis_index("sb"), lax.axis_index("sc")
    group = sa * nc + sb
    heads, rows, e = acc_q.shape
    half = rows // 2
    entering = (before, after)

    def peer(j):
        return (sa, sb, j)

    def group_peer(g):
        return (g // nc, lax.rem(g, nc), sc)

    landing = ((k_hbm, acc_q), (v_hbm, acc_k), (g_hbm, acc_v), (q_hbm, land_q))

    def load(a, h):
        src, dst = landing[a]
        return pltpu.make_async_copy(
            src.at[:, pl.ds(pl.multiple_of(h * e, e), e)], dst.at[h], load_sem.at[a, h]
        )

    def head_at(i):
        return lax.rem(sc + 1 + i, ns)

    for pair in ((0, 1), (2, 3)):
        @pl.loop(0, heads)
        def _(i):
            for a in pair:
                load(a, head_at(i)).start()

    end_copies = [
        pltpu.make_async_copy(prefix_hbm.at[sc], ends.at[0], end_sem.at[0]),
        pltpu.make_async_copy(suffix_hbm.at[sc], ends.at[1], end_sem.at[1]),
    ]
    for c in end_copies:
        c.start()

    barrier = pltpu.get_barrier_semaphore()

    @pl.loop(1, ns)
    def _(i):
        pl.semaphore_signal(barrier, inc=1, device_id=peer(lax.rem(sc + i, ns)), device_id_type=MESH)

    @pl.loop(1, groups)
    def _(i):
        pl.semaphore_signal(barrier, inc=1, device_id=group_peer(lax.rem(group + i, groups)), device_id_type=MESH)

    pl.semaphore_wait(barrier, ns - 1 + groups - 1)

    def in_copy(w, head, source, target):
        return pltpu.make_async_remote_copy(
            src_ref=local.at[w, head], dst_ref=gathered.at[w, source],
            send_sem=in_send.at[w, head], recv_sem=in_recv.at[w, source],
            device_id=peer(target), device_id_type=MESH,
        )

    def total_copy(w, source, target):
        return pltpu.make_async_remote_copy(
            src_ref=totals.at[w, source], dst_ref=totals.at[w, source],
            send_sem=tot_send.at[w, target], recv_sem=tot_recv.at[w, source],
            device_id=group_peer(target), device_id_type=MESH,
        )

    def out_copy(w, head, target):
        return pltpu.make_async_remote_copy(
            src_ref=gathered.at[w, target], dst_ref=entering[w].at[head],
            send_sem=out_send.at[w, target], recv_sem=out_recv.at[w, head],
            device_id=peer(target), device_id_type=MESH,
        )

    def local_sum(w, left, right, left_t, left2, right2):
        @pl.loop(0, heads)
        def _(i):
            h = head_at(i)
            a, b = left, right
            load(a, h).wait()
            load(b, h).wait()
            x2 = split2(landing[a][1][h])
            y2 = split2(landing[b][1][h])
            left2[h] = x2
            right2[h] = y2
            xt = x2.T
            if left_t is not None:
                left_t[h] = xt
            local[w, h] = fold_columns(fold_rows(mm(xt, y2)))

            if w == 0:

                @pl.when(h != sc)
                def _():
                    in_copy(w, h, sc, h).start()

    local_sum(0, 1, 0, None, v2, k2)
    local_sum(1, 2, 3, gt, g2, q2)

    lower = lax.broadcasted_iota(jnp.int32, (half, half), 0) >= lax.broadcasted_iota(
        jnp.int32, (half, half), 1
    )

    def within_block(h):
        qt[h] = q2[h].T
        top, low = pl.ds(0, half), pl.ds(half, half)

        def three(a2, b2):
            s00 = jnp.where(lower, scores(a2[h, top, :], b2[h, top, :]), 0.0)
            s10 = scores(a2[h, low, :], b2[h, top, :])
            s11 = jnp.where(lower, scores(a2[h, low, :], b2[h, low, :]), 0.0)
            return halves(s00), halves(s10), halves(s11)

        def transposed(xt, parts):
            (h00, l00), (h10, l10), (h11, l11) = parts
            x = xt[h]
            first = mm(
                jnp.concatenate([x, x], axis=1),
                jnp.concatenate([h00, h10, l00, l10], axis=0),
            )
            y = x[:, half:]
            second = mm(
                jnp.concatenate([y, y], axis=1), jnp.concatenate([h11, l11], axis=0)
            )
            return fold_rows(first).T, fold_rows(second).T

        parts = three(g2, v2)
        (h00, l00), (h10, l10), (h11, l11) = parts
        kk = k2[h]
        acc_q[h, top, :] = fold_columns(
            fold_rows(mm(jnp.concatenate([h00, l00], axis=0), kk[:half]))
        )
        wide = jnp.concatenate(
            [jnp.concatenate([h10, h11], axis=1), jnp.concatenate([l10, l11], axis=1)],
            axis=0,
        )
        acc_q[h, low, :] = fold_columns(fold_rows(mm(wide, kk)))
        first, second = transposed(qt, parts)
        acc_k[h, top, :] = first
        acc_k[h, low, :] = second
        first, second = transposed(gt, three(q2, k2))
        acc_v[h, top, :] = first
        acc_v[h, low, :] = second

    def segment(start, count):
        if count == 0:
            return

        @pl.loop(start, start + count)
        def _(h):
            within_block(h)

    def send_next():
        @pl.loop(1, ns)
        def _(i):
            j = lax.rem(sc + i, ns)
            in_copy(0, j, sc, j).wait_send()
            in_copy(1, j, sc, j).start()

    def send_totals(w):
        gathered[w, sc] = local[w, sc]

        @pl.loop(1, ns)
        def _(i):
            j = lax.rem(sc + i, ns)
            in_copy(w, j, j, j).wait_recv()

        total = gathered[w, 0]
        for j in range(1, ns):
            total = total + gathered[w, j]
        totals[w, group] = total

        @pl.loop(1, groups)
        def _(i):
            total_copy(w, group, lax.rem(group + i, groups)).start()

    def send_states(w):
        @pl.loop(1, groups)
        def _(i):
            g = lax.rem(group + i, groups)
            total_copy(w, g, g).wait_recv()

        end_copies[w].wait()
        state = ends[w]
        if w == 0:
            state = state.T
        for g in range(groups):
            use = g < group if w == 0 else g > group
            state = state + jnp.where(use, totals[w, g], 0.0)
        for j in range(ns) if w == 0 else reversed(range(ns)):
            term = gathered[w, j]
            gathered[w, j] = state
            state = state + term
        entering[w][sc] = gathered[w, sc]

        @pl.loop(1, ns)
        def _(i):
            out_copy(w, sc, lax.rem(sc + i, ns)).start()

    done = 0
    for count, step in zip(
        SEGMENTS,
        (
            send_next,
            functools.partial(send_totals, 0),
            functools.partial(send_states, 0),
            functools.partial(send_totals, 1),
            functools.partial(send_states, 1),
        ),
    ):
        segment(done, count)
        done += count
        step()
    segment(done, heads - done)

    def arrived(w, i):
        h = lax.rem(sc - i + ns, ns)

        @pl.when(i > 0)
        def _():
            out_copy(w, h, h).wait_recv()

        return h

    @pl.loop(0, heads)
    def _(i):
        h = arrived(0, i)
        qg[h] = finish(factor, g2[h], acc_q[h], before[h])

    @pl.loop(0, heads)
    def _(i):
        arrived(1, i)

    for w in range(2):
        @pl.loop(1, ns)
        def _(i):
            j = lax.rem(sc + i, ns)
            if w == 1:
                in_copy(w, j, sc, j).wait_send()
            out_copy(w, sc, j).wait_send()

        @pl.loop(1, groups)
        def _(i):
            total_copy(w, group, lax.rem(group + i, groups)).wait_send()


def closing_kernel(
    factor, k2, v2, acc_k, acc_v, after, qg, qg_hbm, kg_hbm, vg_hbm, kg, vg, store_sem
):
    heads, _, e = qg.shape

    def store(o, h):
        src, dst = ((qg, qg_hbm), (kg, kg_hbm), (vg, vg_hbm))[o]
        return pltpu.make_async_copy(
            src.at[h], dst.at[:, pl.ds(pl.multiple_of(h * e, e), e)], store_sem.at[o, h]
        )

    @pl.loop(0, heads)
    def _(h):
        state = after[h]
        kg[h] = finish(factor, v2[h], acc_k[h], state)
        vg[h] = finish(factor, k2[h], acc_v[h], state.T)
        for o in range(3):
            store(o, h).start()

    @pl.loop(0, heads)
    def _(h):
        for o in range(3):
            store(o, h).wait()


def shards(axes, queries, key_rows, value_rows, out_grad, prefix_state, suffix_state):
    rows = queries.shape[0]
    heads, e, _ = prefix_state.shape
    nx, nc, ns = axes
    groups = nx * nc
    factor = 1.0 / math.sqrt(e * rows * groups * ns)
    hbm = pl.BlockSpec(memory_space=pl.ANY)
    vmem = pl.BlockSpec(memory_space=pltpu.VMEM)
    dma = pltpu.SemaphoreType.DMA
    pair = pltpu.VMEM((heads, rows, 2 * e), BF16)
    pair_t = pltpu.VMEM((heads, 2 * e, rows), BF16)
    wide = pltpu.VMEM((heads, rows, e), F32)
    one = pltpu.VMEM((heads, e, e), F32)
    states = pltpu.VMEM((2, heads, e, e), F32)
    narrow = pltpu.VMEM((heads, rows, e), BF16)
    kept = pl.pallas_call(
        functools.partial(kernel, axes, factor),
        out_shape=(pair, pair, wide, wide, one, narrow),
        in_specs=[hbm] * 6,
        out_specs=(vmem,) * 6,
        scratch_shapes=[
            pair, pair, pair_t, pair_t, wide, wide,
            states, states, pltpu.VMEM((2, groups, e, e), F32), one,
            pltpu.VMEM((2, e, e), F32),
            dma((4, heads)), dma((2,)),
            dma((2, ns)), dma((2, ns)),
            dma((2, groups)), dma((2, groups)),
            dma((2, ns)), dma((2, ns)),
        ],
        compiler_params=pltpu.CompilerParams(
            collective_id=0, has_side_effects=True, vmem_limit_bytes=36 << 20
        ),
    )(queries, key_rows, value_rows, out_grad, prefix_state, suffix_state)
    out = jax.ShapeDtypeStruct((rows, heads * e), BF16)
    return pl.pallas_call(
        functools.partial(closing_kernel, factor),
        out_shape=(out, out, out),
        in_specs=[vmem] * 6,
        out_specs=(hbm, hbm, hbm),
        scratch_shapes=[narrow, narrow, dma((3, heads))],
        compiler_params=pltpu.CompilerParams(vmem_limit_bytes=6 << 20),
    )(*kept)


def solution(mesh):
    axes = tuple(mesh.shape[name] for name in ("sa", "sb", "sc"))
    split = P(("sa", "sb", "sc"), None)
    return jax.shard_map(
        functools.partial(shards, axes),
        mesh=mesh,
        in_specs=(split, split, split, split, P(), P()),
        out_specs=(split, split, split),
        check_vma=False,
    )
```

```python
import functools
import math

import jax
import jax.numpy as jnp
from jax import lax
from jax.experimental import pallas as pl
from jax.experimental.pallas import tpu as pltpu
from jax.sharding import PartitionSpec as P

MESH = pl.DeviceIdType.MESH
F32 = jnp.float32
BF16 = jnp.bfloat16
SEGMENTS = (1, 2, 6, 1, 6)


def split2(x):
    hi = x.astype(BF16)
    lo = (x - hi.astype(F32)).astype(BF16)
    return jnp.concatenate([hi, lo], axis=1)


def halves(x):
    hi = x.astype(BF16)
    lo = (x - hi.astype(F32)).astype(BF16)
    return hi, lo


def mm(a, b):
    return jnp.dot(a, b, preferred_element_type=F32)


def mm_nt(a, b):
    return lax.dot_general(a, b, (((1,), (1,)), ((), ())), preferred_element_type=F32)


def fold_columns(r):
    n = r.shape[1] // 2
    return r[:, :n] + r[:, n:]


def fold_rows(r):
    n = r.shape[0] // 2
    return r[:n] + r[n:]


def scores(a2, b2):
    e = a2.shape[1] // 2
    swapped = jnp.concatenate([b2[:, e:], b2[:, :e]], axis=1)
    return mm_nt(
        jnp.concatenate([a2, a2], axis=1), jnp.concatenate([b2, swapped], axis=1)
    )


def finish(factor, x2, acc, state):
    s2 = split2(state)
    r = fold_columns(mm(x2, jnp.concatenate([s2, s2], axis=0)))
    return ((r + acc) * factor).astype(BF16)


def kernel(
    axes, factor,
    q_hbm, k_hbm, v_hbm, g_hbm, prefix_hbm, suffix_hbm,
    qg, kg, vg,
    q2, k2, v2, g2, qt, gt, acc_q, acc_k, acc_v, land_q,
    local, gathered, totals, before, after, ends,
    load_sem, end_sem, in_send, in_recv, tot_send, tot_recv, out_send, out_recv,
):
    nx, nc, ns = axes
    groups = nx * nc
    sa, sb, sc = lax.axis_index("sa"), lax.axis_index("sb"), lax.axis_index("sc")
    group = sa * nc + sb
    heads, rows, e = acc_q.shape
    half = rows // 2
    entering = (before, after)

    def peer(j):
        return (sa, sb, j)

    def group_peer(g):
        return (g // nc, lax.rem(g, nc), sc)

    landing = ((k_hbm, acc_q), (v_hbm, acc_k), (g_hbm, acc_v), (q_hbm, land_q))

    def load(a, h):
        src, dst = landing[a]
        return pltpu.make_async_copy(
            src.at[:, pl.ds(pl.multiple_of(h * e, e), e)], dst.at[h], load_sem.at[a, h]
        )

    def head_at(i):
        return lax.rem(sc + 1 + i, ns)

    for pair in ((0, 1), (2, 3)):
        @pl.loop(0, heads)
        def _(i):
            for a in pair:
                load(a, head_at(i)).start()

    end_copies = [
        pltpu.make_async_copy(prefix_hbm.at[sc], ends.at[0], end_sem.at[0]),
        pltpu.make_async_copy(suffix_hbm.at[sc], ends.at[1], end_sem.at[1]),
    ]
    for c in end_copies:
        c.start()

    barrier = pltpu.get_barrier_semaphore()

    @pl.loop(1, ns)
    def _(i):
        pl.semaphore_signal(barrier, inc=1, device_id=peer(lax.rem(sc + i, ns)), device_id_type=MESH)

    @pl.loop(1, groups)
    def _(i):
        pl.semaphore_signal(barrier, inc=1, device_id=group_peer(lax.rem(group + i, groups)), device_id_type=MESH)

    pl.semaphore_wait(barrier, ns - 1 + groups - 1)

    def in_copy(w, head, source, target):
        return pltpu.make_async_remote_copy(
            src_ref=local.at[w, head], dst_ref=gathered.at[w, source],
            send_sem=in_send.at[w, head], recv_sem=in_recv.at[w, source],
            device_id=peer(target), device_id_type=MESH,
        )

    def total_copy(w, source, target):
        return pltpu.make_async_remote_copy(
            src_ref=totals.at[w, source], dst_ref=totals.at[w, source],
            send_sem=tot_send.at[w, target], recv_sem=tot_recv.at[w, source],
            device_id=group_peer(target), device_id_type=MESH,
        )

    def out_copy(w, head, target):
        return pltpu.make_async_remote_copy(
            src_ref=gathered.at[w, target], dst_ref=entering[w].at[head],
            send_sem=out_send.at[w, target], recv_sem=out_recv.at[w, head],
            device_id=peer(target), device_id_type=MESH,
        )

    def local_sum(w, left, right, left_t, left2, right2):
        @pl.loop(0, heads)
        def _(i):
            h = head_at(i)
            a, b = left, right
            load(a, h).wait()
            load(b, h).wait()
            x2 = split2(landing[a][1][h])
            y2 = split2(landing[b][1][h])
            left2[h] = x2
            right2[h] = y2
            xt = x2.T
            if left_t is not None:
                left_t[h] = xt
            local[w, h] = fold_columns(fold_rows(mm(xt, y2)))

            if w == 0:

                @pl.when(h != sc)
                def _():
                    in_copy(w, h, sc, h).start()

    local_sum(0, 1, 0, None, v2, k2)
    local_sum(1, 2, 3, gt, g2, q2)

    lower = lax.broadcasted_iota(jnp.int32, (half, half), 0) >= lax.broadcasted_iota(
        jnp.int32, (half, half), 1
    )

    def within_block(h):
        qt[h] = q2[h].T
        top, low = pl.ds(0, half), pl.ds(half, half)

        def three(a2, b2):
            s00 = jnp.where(lower, scores(a2[h, top, :], b2[h, top, :]), 0.0)
            s10 = scores(a2[h, low, :], b2[h, top, :])
            s11 = jnp.where(lower, scores(a2[h, low, :], b2[h, low, :]), 0.0)
            return halves(s00), halves(s10), halves(s11)

        def transposed(xt, parts):
            (h00, l00), (h10, l10), (h11, l11) = parts
            x = xt[h]
            first = mm(
                jnp.concatenate([x, x], axis=1),
                jnp.concatenate([h00, h10, l00, l10], axis=0),
            )
            y = x[:, half:]
            second = mm(
                jnp.concatenate([y, y], axis=1), jnp.concatenate([h11, l11], axis=0)
            )
            return fold_rows(first).T, fold_rows(second).T

        parts = three(g2, v2)
        (h00, l00), (h10, l10), (h11, l11) = parts
        kk = k2[h]
        acc_q[h, top, :] = fold_columns(
            fold_rows(mm(jnp.concatenate([h00, l00], axis=0), kk[:half]))
        )
        wide = jnp.concatenate(
            [jnp.concatenate([h10, h11], axis=1), jnp.concatenate([l10, l11], axis=1)],
            axis=0,
        )
        acc_q[h, low, :] = fold_columns(fold_rows(mm(wide, kk)))
        first, second = transposed(qt, parts)
        acc_k[h, top, :] = first
        acc_k[h, low, :] = second
        first, second = transposed(gt, three(q2, k2))
        acc_v[h, top, :] = first
        acc_v[h, low, :] = second

    def segment(start, count):
        if count == 0:
            return

        @pl.loop(start, start + count)
        def _(h):
            within_block(h)

    def send_next():
        @pl.loop(1, ns)
        def _(i):
            j = lax.rem(sc + i, ns)
            in_copy(0, j, sc, j).wait_send()
            in_copy(1, j, sc, j).start()

    def send_totals(w):
        gathered[w, sc] = local[w, sc]

        @pl.loop(1, ns)
        def _(i):
            j = lax.rem(sc + i, ns)
            in_copy(w, j, j, j).wait_recv()

        total = gathered[w, 0]
        for j in range(1, ns):
            total = total + gathered[w, j]
        totals[w, group] = total

        @pl.loop(1, groups)
        def _(i):
            total_copy(w, group, lax.rem(group + i, groups)).start()

    def send_states(w):
        @pl.loop(1, groups)
        def _(i):
            g = lax.rem(group + i, groups)
            total_copy(w, g, g).wait_recv()

        end_copies[w].wait()
        state = ends[w]
        if w == 0:
            state = state.T
        for g in range(groups):
            use = g < group if w == 0 else g > group
            state = state + jnp.where(use, totals[w, g], 0.0)
        for j in range(ns) if w == 0 else reversed(range(ns)):
            term = gathered[w, j]
            gathered[w, j] = state
            state = state + term
        entering[w][sc] = gathered[w, sc]

        @pl.loop(1, ns)
        def _(i):
            out_copy(w, sc, lax.rem(sc + i, ns)).start()

    done = 0
    for count, step in zip(
        SEGMENTS,
        (
            send_next,
            functools.partial(send_totals, 0),
            functools.partial(send_states, 0),
            functools.partial(send_totals, 1),
            functools.partial(send_states, 1),
        ),
    ):
        segment(done, count)
        done += count
        step()
    segment(done, heads - done)

    def arrived(w, i):
        h = lax.rem(sc - i + ns, ns)

        @pl.when(i > 0)
        def _():
            out_copy(w, h, h).wait_recv()

        return h

    @pl.loop(0, heads)
    def _(i):
        h = arrived(0, i)
        qg[h] = finish(factor, g2[h], acc_q[h], before[h])

    @pl.loop(0, heads)
    def _(i):
        h = arrived(1, i)
        state = after[h]
        kg[h] = finish(factor, v2[h], acc_k[h], state)
        vg[h] = finish(factor, k2[h], acc_v[h], state.T)

    for w in range(2):
        @pl.loop(1, ns)
        def _(i):
            j = lax.rem(sc + i, ns)
            if w == 1:
                in_copy(w, j, sc, j).wait_send()
            out_copy(w, sc, j).wait_send()

        @pl.loop(1, groups)
        def _(i):
            total_copy(w, group, lax.rem(group + i, groups)).wait_send()


def store_kernel(qg, kg, vg, qg_hbm, kg_hbm, vg_hbm, store_sem):
    heads, _, e = qg.shape
    copies = [
        pltpu.make_async_copy(src.at[h], dst.at[:, pl.ds(h * e, e)], store_sem.at[o, h])
        for o, (src, dst) in enumerate(((qg, qg_hbm), (kg, kg_hbm), (vg, vg_hbm)))
        for h in range(heads)
    ]
    for c in copies:
        c.start()
    for c in copies:
        c.wait()


def shards(axes, queries, key_rows, value_rows, out_grad, prefix_state, suffix_state):
    rows = queries.shape[0]
    heads, e, _ = prefix_state.shape
    nx, nc, ns = axes
    groups = nx * nc
    factor = 1.0 / math.sqrt(e * rows * groups * ns)
    hbm = pl.BlockSpec(memory_space=pl.ANY)
    vmem = pl.BlockSpec(memory_space=pltpu.VMEM)
    dma = pltpu.SemaphoreType.DMA
    pair = pltpu.VMEM((heads, rows, 2 * e), BF16)
    pair_t = pltpu.VMEM((heads, 2 * e, rows), BF16)
    wide = pltpu.VMEM((heads, rows, e), F32)
    one = pltpu.VMEM((heads, e, e), F32)
    states = pltpu.VMEM((2, heads, e, e), F32)
    narrow = pltpu.VMEM((heads, rows, e), BF16)
    kept = pl.pallas_call(
        functools.partial(kernel, axes, factor),
        out_shape=(narrow,) * 3,
        in_specs=[hbm] * 6,
        out_specs=(vmem,) * 3,
        scratch_shapes=[
            pair, pair, pair, pair, pair_t, pair_t, wide, wide, wide, wide,
            states, states, pltpu.VMEM((2, groups, e, e), F32), one, one,
            pltpu.VMEM((2, e, e), F32),
            dma((4, heads)), dma((2,)),
            dma((2, ns)), dma((2, ns)),
            dma((2, groups)), dma((2, groups)),
            dma((2, ns)), dma((2, ns)),
        ],
        compiler_params=pltpu.CompilerParams(
            collective_id=0, has_side_effects=True, vmem_limit_bytes=52 << 20
        ),
    )(queries, key_rows, value_rows, out_grad, prefix_state, suffix_state)
    out = jax.ShapeDtypeStruct((rows, heads * e), BF16)
    return pl.pallas_call(
        store_kernel,
        out_shape=(out, out, out),
        in_specs=[vmem] * 3,
        out_specs=(hbm, hbm, hbm),
        scratch_shapes=[dma((3, heads))],
        compiler_params=pltpu.CompilerParams(vmem_limit_bytes=2 << 20),
    )(*kept)


def solution(mesh):
    axes = tuple(mesh.shape[name] for name in ("sa", "sb", "sc"))
    split = P(("sa", "sb", "sc"), None)
    return jax.shard_map(
        functools.partial(shards, axes),
        mesh=mesh,
        in_specs=(split, split, split, split, P(), P()),
        out_specs=(split, split, split),
        check_vma=False,
    )
```

```python
import functools
import math

import jax
import jax.numpy as jnp
from jax import lax
from jax.experimental import pallas as pl
from jax.experimental.pallas import tpu as pltpu
from jax.sharding import PartitionSpec as P

MESH = pl.DeviceIdType.MESH
F32 = jnp.float32
BF16 = jnp.bfloat16
SEGMENTS = (1, 2, 6, 1, 6)


def split2(x):
    hi = x.astype(BF16)
    lo = (x - hi.astype(F32)).astype(BF16)
    return jnp.concatenate([hi, lo], axis=1)


def halves(x):
    hi = x.astype(BF16)
    lo = (x - hi.astype(F32)).astype(BF16)
    return hi, lo


def mm(a, b):
    return jnp.dot(a, b, preferred_element_type=F32)


def mm_nt(a, b):
    return lax.dot_general(a, b, (((1,), (1,)), ((), ())), preferred_element_type=F32)


def fold_columns(r):
    n = r.shape[1] // 2
    return r[:, :n] + r[:, n:]


def fold_rows(r):
    n = r.shape[0] // 2
    return r[:n] + r[n:]


def scores(a2, b2):
    e = a2.shape[1] // 2
    swapped = jnp.concatenate([b2[:, e:], b2[:, :e]], axis=1)
    return mm_nt(
        jnp.concatenate([a2, a2], axis=1), jnp.concatenate([b2, swapped], axis=1)
    )


def finish(factor, x2, acc, state):
    s2 = split2(state)
    r = fold_columns(mm(x2, jnp.concatenate([s2, s2], axis=0)))
    return ((r + acc) * factor).astype(BF16)


def kernel(
    axes, factor,
    q_hbm, k_hbm, v_hbm, g_hbm, prefix_hbm, suffix_hbm,
    qg, kg, vg,
    q2, k2, v2, g2, qt, gt, acc_q, acc_k, acc_v, land_q,
    local, gathered, totals, before, after, ends,
    load_sem, end_sem, in_send, in_recv, tot_send, tot_recv, out_send, out_recv,
):
    nx, nc, ns = axes
    groups = nx * nc
    sa, sb, sc = lax.axis_index("sa"), lax.axis_index("sb"), lax.axis_index("sc")
    group = sa * nc + sb
    heads, rows, e = acc_q.shape
    half = rows // 2
    entering = (before, after)

    def peer(j):
        return (sa, sb, j)

    def group_peer(g):
        return (g // nc, lax.rem(g, nc), sc)

    landing = ((k_hbm, acc_q), (v_hbm, acc_k), (g_hbm, acc_v), (q_hbm, land_q))

    def load(a, h):
        src, dst = landing[a]
        return pltpu.make_async_copy(
            src.at[:, pl.ds(pl.multiple_of(h * e, e), e)], dst.at[h], load_sem.at[a, h]
        )

    def head_at(i):
        return lax.rem(sc + 1 + i, ns)

    barrier = pltpu.get_barrier_semaphore()

    @pl.loop(1, ns)
    def _(i):
        pl.semaphore_signal(barrier, inc=1, device_id=peer(lax.rem(sc + i, ns)), device_id_type=MESH)

    @pl.loop(1, groups)
    def _(i):
        pl.semaphore_signal(barrier, inc=1, device_id=group_peer(lax.rem(group + i, groups)), device_id_type=MESH)

    @pl.loop(0, heads)
    def _(i):
        for a in (0, 1):
            load(a, head_at(i)).start()

    end_copies = [
        pltpu.make_async_copy(prefix_hbm.at[sc], ends.at[0], end_sem.at[0]),
        pltpu.make_async_copy(suffix_hbm.at[sc], ends.at[1], end_sem.at[1]),
    ]
    for c in end_copies:
        c.start()

    pl.semaphore_wait(barrier, ns - 1 + groups - 1)

    def in_copy(w, head, source, target):
        return pltpu.make_async_remote_copy(
            src_ref=local.at[w, head], dst_ref=gathered.at[w, source],
            send_sem=in_send.at[w, head], recv_sem=in_recv.at[w, source],
            device_id=peer(target), device_id_type=MESH,
        )

    def total_copy(w, source, target):
        return pltpu.make_async_remote_copy(
            src_ref=totals.at[w, source], dst_ref=totals.at[w, source],
            send_sem=tot_send.at[w, target], recv_sem=tot_recv.at[w, source],
            device_id=group_peer(target), device_id_type=MESH,
        )

    def out_copy(w, head, target):
        return pltpu.make_async_remote_copy(
            src_ref=gathered.at[w, target], dst_ref=entering[w].at[head],
            send_sem=out_send.at[w, target], recv_sem=out_recv.at[w, head],
            device_id=peer(target), device_id_type=MESH,
        )

    def local_sum(w, left, right, left_t, left2, right2):
        @pl.loop(0, heads)
        def _(i):
            h = head_at(i)
            a, b = left, right
            if w == 0:
                for later in (2, 3):
                    load(later, h).start()
            load(a, h).wait()
            load(b, h).wait()
            x2 = split2(landing[a][1][h])
            y2 = split2(landing[b][1][h])
            left2[h] = x2
            right2[h] = y2
            xt = x2.T
            if left_t is not None:
                left_t[h] = xt
            local[w, h] = fold_columns(fold_rows(mm(xt, y2)))

            if w == 0:

                @pl.when(h != sc)
                def _():
                    in_copy(w, h, sc, h).start()

    local_sum(0, 1, 0, None, v2, k2)
    local_sum(1, 2, 3, gt, g2, q2)

    lower = lax.broadcasted_iota(jnp.int32, (half, half), 0) >= lax.broadcasted_iota(
        jnp.int32, (half, half), 1
    )

    def within_block(h):
        qt[h] = q2[h].T
        top, low = pl.ds(0, half), pl.ds(half, half)

        def three(a2, b2):
            s00 = jnp.where(lower, scores(a2[h, top, :], b2[h, top, :]), 0.0)
            s10 = scores(a2[h, low, :], b2[h, top, :])
            s11 = jnp.where(lower, scores(a2[h, low, :], b2[h, low, :]), 0.0)
            return halves(s00), halves(s10), halves(s11)

        def transposed(xt, parts):
            (h00, l00), (h10, l10), (h11, l11) = parts
            x = xt[h]
            first = mm(
                jnp.concatenate([x, x], axis=1),
                jnp.concatenate([h00, h10, l00, l10], axis=0),
            )
            y = x[:, half:]
            second = mm(
                jnp.concatenate([y, y], axis=1), jnp.concatenate([h11, l11], axis=0)
            )
            return fold_rows(first).T, fold_rows(second).T

        parts = three(g2, v2)
        (h00, l00), (h10, l10), (h11, l11) = parts
        kk = k2[h]
        acc_q[h, top, :] = fold_columns(
            fold_rows(mm(jnp.concatenate([h00, l00], axis=0), kk[:half]))
        )
        wide = jnp.concatenate(
            [jnp.concatenate([h10, h11], axis=1), jnp.concatenate([l10, l11], axis=1)],
            axis=0,
        )
        acc_q[h, low, :] = fold_columns(fold_rows(mm(wide, kk)))
        first, second = transposed(qt, parts)
        acc_k[h, top, :] = first
        acc_k[h, low, :] = second
        first, second = transposed(gt, three(q2, k2))
        acc_v[h, top, :] = first
        acc_v[h, low, :] = second

    def segment(start, count):
        if count == 0:
            return

        @pl.loop(start, start + count)
        def _(h):
            within_block(h)

    def send_next():
        @pl.loop(1, ns)
        def _(i):
            j = lax.rem(sc + i, ns)
            in_copy(0, j, sc, j).wait_send()
            in_copy(1, j, sc, j).start()

    def send_totals(w):
        gathered[w, sc] = local[w, sc]

        @pl.loop(1, ns)
        def _(i):
            j = lax.rem(sc + i, ns)
            in_copy(w, j, j, j).wait_recv()

        total = gathered[w, 0]
        for j in range(1, ns):
            total = total + gathered[w, j]
        totals[w, group] = total

        @pl.loop(1, groups)
        def _(i):
            total_copy(w, group, lax.rem(group + i, groups)).start()

    def send_states(w):
        @pl.loop(1, groups)
        def _(i):
            g = lax.rem(group + i, groups)
            total_copy(w, g, g).wait_recv()

        end_copies[w].wait()
        state = ends[w]
        if w == 0:
            state = state.T
        for g in range(groups):
            use = g < group if w == 0 else g > group
            state = state + jnp.where(use, totals[w, g], 0.0)
        for j in range(ns) if w == 0 else reversed(range(ns)):
            term = gathered[w, j]
            gathered[w, j] = state
            state = state + term
        entering[w][sc] = gathered[w, sc]

        @pl.loop(1, ns)
        def _(i):
            out_copy(w, sc, lax.rem(sc + i, ns)).start()

    done = 0
    for count, step in zip(
        SEGMENTS,
        (
            send_next,
            functools.partial(send_totals, 0),
            functools.partial(send_states, 0),
            functools.partial(send_totals, 1),
            functools.partial(send_states, 1),
        ),
    ):
        segment(done, count)
        done += count
        step()
    segment(done, heads - done)

    def arrived(w, i):
        h = lax.rem(sc - i + ns, ns)

        @pl.when(i > 0)
        def _():
            out_copy(w, h, h).wait_recv()

        return h

    @pl.loop(0, heads)
    def _(i):
        h = arrived(0, i)
        qg[h] = finish(factor, g2[h], acc_q[h], before[h])

    @pl.loop(0, heads)
    def _(i):
        h = arrived(1, i)
        state = after[h]
        kg[h] = finish(factor, v2[h], acc_k[h], state)
        vg[h] = finish(factor, k2[h], acc_v[h], state.T)

    for w in range(2):
        @pl.loop(1, ns)
        def _(i):
            j = lax.rem(sc + i, ns)
            if w == 1:
                in_copy(w, j, sc, j).wait_send()
            out_copy(w, sc, j).wait_send()

        @pl.loop(1, groups)
        def _(i):
            total_copy(w, group, lax.rem(group + i, groups)).wait_send()


def store_kernel(qg, kg, vg, qg_hbm, kg_hbm, vg_hbm, store_sem):
    heads, _, e = qg.shape
    copies = [
        pltpu.make_async_copy(src.at[h], dst.at[:, pl.ds(h * e, e)], store_sem.at[o, h])
        for o, (src, dst) in enumerate(((qg, qg_hbm), (kg, kg_hbm), (vg, vg_hbm)))
        for h in range(heads)
    ]
    for c in copies:
        c.start()
    for c in copies:
        c.wait()


def shards(axes, queries, key_rows, value_rows, out_grad, prefix_state, suffix_state):
    rows = queries.shape[0]
    heads, e, _ = prefix_state.shape
    nx, nc, ns = axes
    groups = nx * nc
    factor = 1.0 / math.sqrt(e * rows * groups * ns)
    hbm = pl.BlockSpec(memory_space=pl.ANY)
    vmem = pl.BlockSpec(memory_space=pltpu.VMEM)
    dma = pltpu.SemaphoreType.DMA
    pair = pltpu.VMEM((heads, rows, 2 * e), BF16)
    pair_t = pltpu.VMEM((heads, 2 * e, rows), BF16)
    wide = pltpu.VMEM((heads, rows, e), F32)
    one = pltpu.VMEM((heads, e, e), F32)
    states = pltpu.VMEM((2, heads, e, e), F32)
    narrow = pltpu.VMEM((heads, rows, e), BF16)
    kept = pl.pallas_call(
        functools.partial(kernel, axes, factor),
        out_shape=(narrow,) * 3,
        in_specs=[hbm] * 6,
        out_specs=(vmem,) * 3,
        scratch_shapes=[
            pair, pair, pair, pair, pair_t, pair_t, wide, wide, wide, wide,
            states, states, pltpu.VMEM((2, groups, e, e), F32), one, one,
            pltpu.VMEM((2, e, e), F32),
            dma((4, heads)), dma((2,)),
            dma((2, ns)), dma((2, ns)),
            dma((2, groups)), dma((2, groups)),
            dma((2, ns)), dma((2, ns)),
        ],
        compiler_params=pltpu.CompilerParams(
            collective_id=0, has_side_effects=True, vmem_limit_bytes=52 << 20
        ),
    )(queries, key_rows, value_rows, out_grad, prefix_state, suffix_state)
    out = jax.ShapeDtypeStruct((rows, heads * e), BF16)
    return pl.pallas_call(
        store_kernel,
        out_shape=(out, out, out),
        in_specs=[vmem] * 3,
        out_specs=(hbm, hbm, hbm),
        scratch_shapes=[dma((3, heads))],
        compiler_params=pltpu.CompilerParams(vmem_limit_bytes=2 << 20),
    )(*kept)


def solution(mesh):
    axes = tuple(mesh.shape[name] for name in ("sa", "sb", "sc"))
    split = P(("sa", "sb", "sc"), None)
    return jax.shard_map(
        functools.partial(shards, axes),
        mesh=mesh,
        in_specs=(split, split, split, split, P(), P()),
        out_specs=(split, split, split),
        check_vma=False,
    )
```

```python
import functools
import math

import jax
import jax.numpy as jnp
from jax import lax
from jax.experimental import pallas as pl
from jax.experimental.pallas import tpu as pltpu
from jax.sharding import PartitionSpec as P

MESH = pl.DeviceIdType.MESH
F32 = jnp.float32
BF16 = jnp.bfloat16
SEGMENTS = (0, 2, 6, 1, 6)


def split2(x):
    hi = x.astype(BF16)
    lo = (x - hi.astype(F32)).astype(BF16)
    return jnp.concatenate([hi, lo], axis=1)


def halves(x):
    hi = x.astype(BF16)
    lo = (x - hi.astype(F32)).astype(BF16)
    return hi, lo


def mm(a, b):
    return jnp.dot(a, b, preferred_element_type=F32)


def mm_nt(a, b):
    return lax.dot_general(a, b, (((1,), (1,)), ((), ())), preferred_element_type=F32)


def fold_columns(r):
    n = r.shape[1] // 2
    return r[:, :n] + r[:, n:]


def fold_rows(r):
    n = r.shape[0] // 2
    return r[:n] + r[n:]


def scores(a2, b2):
    e = a2.shape[1] // 2
    swapped = jnp.concatenate([b2[:, e:], b2[:, :e]], axis=1)
    return mm_nt(
        jnp.concatenate([a2, a2], axis=1), jnp.concatenate([b2, swapped], axis=1)
    )


def finish(factor, x2, acc, state):
    s2 = split2(state)
    r = fold_columns(mm(x2, jnp.concatenate([s2, s2], axis=0)))
    return ((r + acc) * factor).astype(BF16)


def kernel(
    axes, factor,
    q_hbm, k_hbm, v_hbm, g_hbm, prefix_hbm, suffix_hbm,
    qg, kg, vg,
    q2, k2, v2, g2, qt, gt, acc_q, acc_k, acc_v, land_q,
    local, gathered, totals, before, after, ends,
    load_sem, end_sem, in_send, in_recv, tot_send, tot_recv, out_send, out_recv,
):
    nx, nc, ns = axes
    groups = nx * nc
    sa, sb, sc = lax.axis_index("sa"), lax.axis_index("sb"), lax.axis_index("sc")
    group = sa * nc + sb
    heads, rows, e = acc_q.shape
    half = rows // 2
    entering = (before, after)

    def peer(j):
        return (sa, sb, j)

    def group_peer(g):
        return (g // nc, lax.rem(g, nc), sc)

    landing = ((k_hbm, acc_q), (v_hbm, acc_k), (g_hbm, acc_v), (q_hbm, land_q))

    def load(a, h):
        src, dst = landing[a]
        return pltpu.make_async_copy(
            src.at[:, pl.ds(pl.multiple_of(h * e, e), e)], dst.at[h], load_sem.at[a, h]
        )

    def head_at(i):
        return lax.rem(sc + 1 + i, ns)

    for pair in ((0, 1), (2, 3)):
        @pl.loop(0, heads)
        def _(i):
            for a in pair:
                load(a, head_at(i)).start()

    end_copies = [
        pltpu.make_async_copy(prefix_hbm.at[sc], ends.at[0], end_sem.at[0]),
        pltpu.make_async_copy(suffix_hbm.at[sc], ends.at[1], end_sem.at[1]),
    ]
    for c in end_copies:
        c.start()

    barrier = pltpu.get_barrier_semaphore()

    @pl.loop(1, ns)
    def _(i):
        pl.semaphore_signal(barrier, inc=1, device_id=peer(lax.rem(sc + i, ns)), device_id_type=MESH)

    @pl.loop(1, groups)
    def _(i):
        pl.semaphore_signal(barrier, inc=1, device_id=group_peer(lax.rem(group + i, groups)), device_id_type=MESH)

    pl.semaphore_wait(barrier, ns - 1 + groups - 1)

    def in_copy(w, head, source, target):
        return pltpu.make_async_remote_copy(
            src_ref=local.at[w, head], dst_ref=gathered.at[w, source],
            send_sem=in_send.at[w, head], recv_sem=in_recv.at[w, source],
            device_id=peer(target), device_id_type=MESH,
        )

    def total_copy(w, source, target):
        return pltpu.make_async_remote_copy(
            src_ref=totals.at[w, source], dst_ref=totals.at[w, source],
            send_sem=tot_send.at[w, target], recv_sem=tot_recv.at[w, source],
            device_id=group_peer(target), device_id_type=MESH,
        )

    def out_copy(w, head, target):
        return pltpu.make_async_remote_copy(
            src_ref=gathered.at[w, target], dst_ref=entering[w].at[head],
            send_sem=out_send.at[w, target], recv_sem=out_recv.at[w, head],
            device_id=peer(target), device_id_type=MESH,
        )

    def local_sum(w, left, right, left_t, left2, right2):
        @pl.loop(0, heads)
        def _(i):
            h = head_at(i)
            a, b = left, right
            load(a, h).wait()
            load(b, h).wait()
            x2 = split2(landing[a][1][h])
            y2 = split2(landing[b][1][h])
            left2[h] = x2
            right2[h] = y2
            xt = x2.T
            if left_t is not None:
                left_t[h] = xt
            local[w, h] = fold_columns(fold_rows(mm(xt, y2)))

            if w == 0:

                @pl.when(h != sc)
                def _():
                    in_copy(w, h, sc, h).start()

    local_sum(0, 1, 0, None, v2, k2)
    local_sum(1, 2, 3, gt, g2, q2)

    lower = lax.broadcasted_iota(jnp.int32, (half, half), 0) >= lax.broadcasted_iota(
        jnp.int32, (half, half), 1
    )

    def within_block(h):
        qt[h] = q2[h].T
        top, low = pl.ds(0, half), pl.ds(half, half)

        def three(a2, b2):
            s00 = jnp.where(lower, scores(a2[h, top, :], b2[h, top, :]), 0.0)
            s10 = scores(a2[h, low, :], b2[h, top, :])
            s11 = jnp.where(lower, scores(a2[h, low, :], b2[h, low, :]), 0.0)
            return halves(s00), halves(s10), halves(s11)

        def transposed(xt, parts):
            (h00, l00), (h10, l10), (h11, l11) = parts
            x = xt[h]
            first = mm(
                jnp.concatenate([x, x], axis=1),
                jnp.concatenate([h00, h10, l00, l10], axis=0),
            )
            y = x[:, half:]
            second = mm(
                jnp.concatenate([y, y], axis=1), jnp.concatenate([h11, l11], axis=0)
            )
            return fold_rows(first).T, fold_rows(second).T

        parts = three(g2, v2)
        (h00, l00), (h10, l10), (h11, l11) = parts
        kk = k2[h]
        acc_q[h, top, :] = fold_columns(
            fold_rows(mm(jnp.concatenate([h00, l00], axis=0), kk[:half]))
        )
        wide = jnp.concatenate(
            [jnp.concatenate([h10, h11], axis=1), jnp.concatenate([l10, l11], axis=1)],
            axis=0,
        )
        acc_q[h, low, :] = fold_columns(fold_rows(mm(wide, kk)))
        first, second = transposed(qt, parts)
        acc_k[h, top, :] = first
        acc_k[h, low, :] = second
        first, second = transposed(gt, three(q2, k2))
        acc_v[h, top, :] = first
        acc_v[h, low, :] = second

    def segment(start, count):
        if count == 0:
            return

        @pl.loop(start, start + count)
        def _(h):
            within_block(h)

    def send_next():
        @pl.loop(1, ns)
        def _(i):
            j = lax.rem(sc + i, ns)
            in_copy(0, j, sc, j).wait_send()
            in_copy(1, j, sc, j).start()

    def send_totals(w):
        gathered[w, sc] = local[w, sc]

        @pl.loop(1, ns)
        def _(i):
            j = lax.rem(sc + i, ns)
            in_copy(w, j, j, j).wait_recv()

        total = gathered[w, 0]
        for j in range(1, ns):
            total = total + gathered[w, j]
        totals[w, group] = total

        @pl.loop(1, groups)
        def _(i):
            total_copy(w, group, lax.rem(group + i, groups)).start()

    def send_states(w):
        @pl.loop(1, groups)
        def _(i):
            g = lax.rem(group + i, groups)
            total_copy(w, g, g).wait_recv()

        end_copies[w].wait()
        state = ends[w]
        if w == 0:
            state = state.T
        for g in range(groups):
            use = g < group if w == 0 else g > group
            state = state + jnp.where(use, totals[w, g], 0.0)
        for j in range(ns) if w == 0 else reversed(range(ns)):
            term = gathered[w, j]
            gathered[w, j] = state
            state = state + term
        entering[w][sc] = gathered[w, sc]

        @pl.loop(1, ns)
        def _(i):
            out_copy(w, sc, lax.rem(sc + i, ns)).start()

    done = 0
    for count, step in zip(
        SEGMENTS,
        (
            send_next,
            functools.partial(send_totals, 0),
            functools.partial(send_states, 0),
            functools.partial(send_totals, 1),
            functools.partial(send_states, 1),
        ),
    ):
        segment(done, count)
        done += count
        step()
    segment(done, heads - done)

    def arrived(w, i):
        h = lax.rem(sc - i + ns, ns)

        @pl.when(i > 0)
        def _():
            out_copy(w, h, h).wait_recv()

        return h

    @pl.loop(0, heads)
    def _(i):
        h = arrived(0, i)
        qg[h] = finish(factor, g2[h], acc_q[h], before[h])

    @pl.loop(0, heads)
    def _(i):
        h = arrived(1, i)
        state = after[h]
        kg[h] = finish(factor, v2[h], acc_k[h], state)
        vg[h] = finish(factor, k2[h], acc_v[h], state.T)

    for w in range(2):
        @pl.loop(1, ns)
        def _(i):
            j = lax.rem(sc + i, ns)
            if w == 1:
                in_copy(w, j, sc, j).wait_send()
            out_copy(w, sc, j).wait_send()

        @pl.loop(1, groups)
        def _(i):
            total_copy(w, group, lax.rem(group + i, groups)).wait_send()


def store_kernel(qg, kg, vg, qg_hbm, kg_hbm, vg_hbm, store_sem):
    heads, _, e = qg.shape
    copies = [
        pltpu.make_async_copy(src.at[h], dst.at[:, pl.ds(h * e, e)], store_sem.at[o, h])
        for o, (src, dst) in enumerate(((qg, qg_hbm), (kg, kg_hbm), (vg, vg_hbm)))
        for h in range(heads)
    ]
    for c in copies:
        c.start()
    for c in copies:
        c.wait()


def shards(axes, queries, key_rows, value_rows, out_grad, prefix_state, suffix_state):
    rows = queries.shape[0]
    heads, e, _ = prefix_state.shape
    nx, nc, ns = axes
    groups = nx * nc
    factor = 1.0 / math.sqrt(e * rows * groups * ns)
    hbm = pl.BlockSpec(memory_space=pl.ANY)
    vmem = pl.BlockSpec(memory_space=pltpu.VMEM)
    dma = pltpu.SemaphoreType.DMA
    pair = pltpu.VMEM((heads, rows, 2 * e), BF16)
    pair_t = pltpu.VMEM((heads, 2 * e, rows), BF16)
    wide = pltpu.VMEM((heads, rows, e), F32)
    one = pltpu.VMEM((heads, e, e), F32)
    states = pltpu.VMEM((2, heads, e, e), F32)
    narrow = pltpu.VMEM((heads, rows, e), BF16)
    kept = pl.pallas_call(
        functools.partial(kernel, axes, factor),
        out_shape=(narrow,) * 3,
        in_specs=[hbm] * 6,
        out_specs=(vmem,) * 3,
        scratch_shapes=[
            pair, pair, pair, pair, pair_t, pair_t, wide, wide, wide, wide,
            states, states, pltpu.VMEM((2, groups, e, e), F32), one, one,
            pltpu.VMEM((2, e, e), F32),
            dma((4, heads)), dma((2,)),
            dma((2, ns)), dma((2, ns)),
            dma((2, groups)), dma((2, groups)),
            dma((2, ns)), dma((2, ns)),
        ],
        compiler_params=pltpu.CompilerParams(
            collective_id=0, has_side_effects=True, vmem_limit_bytes=52 << 20
        ),
    )(queries, key_rows, value_rows, out_grad, prefix_state, suffix_state)
    out = jax.ShapeDtypeStruct((rows, heads * e), BF16)
    return pl.pallas_call(
        store_kernel,
        out_shape=(out, out, out),
        in_specs=[vmem] * 3,
        out_specs=(hbm, hbm, hbm),
        scratch_shapes=[dma((3, heads))],
        compiler_params=pltpu.CompilerParams(vmem_limit_bytes=2 << 20),
    )(*kept)


def solution(mesh):
    axes = tuple(mesh.shape[name] for name in ("sa", "sb", "sc"))
    split = P(("sa", "sb", "sc"), None)
    return jax.shard_map(
        functools.partial(shards, axes),
        mesh=mesh,
        in_specs=(split, split, split, split, P(), P()),
        out_specs=(split, split, split),
        check_vma=False,
    )
```
